128 devices in a mesh: band: 8 (over y_lo, z), dom: 16 (over x, y_hi, core).
Axes of the slice: x: 4, y: 4 (y_hi: 2, y_lo: 2; y = y_hi * 2 + y_lo), z: 4, core: 2. Of those that a mesh axis runs over, the one named last changes fastest.
Arguments:
- orbitals: bfloat16 [64, 32, 128, 256], P('band', 'dom'), may hold values from -6 to 6
- visit_blocks: int32 [2], replicated, may hold values from 0 to 15, as said below
- kernel_rates: float32 [3], replicated, may hold values from 0.0098 to 3.41
- kernel_weights: float32 [3], replicated, may hold values from 0.07 to 1.42
Outputs:
- exchange_terms: float32 [64, 32, 128, 256], P('band', 'dom')
The draws below stay inside these ranges and needn't reach their ends.
Inputs may be any that keep to these rules, and one draw needn't show every extreme that they name: Entry k names band group visit_blocks[k] // 2 and the half visit_blocks[k] % 2 of its orbitals; the entries are distinct, and one of them names the second half of the last band group.
All inputs are finite; a program needn't handle non-finite values.
Results may differ from the reference program's by a relative error of at most 0.0023.
Values may be sent and summed in bfloat16 or wider, within the bound.
A program may use at most 192 MiB of HBM per device.

```python
import jax
import jax.numpy as jnp
from jax import lax

CY = 128
CZ = 256
RESIDENT = 8
BLOCK = 4
VISITS = 2
GAUSS = 3
REACH = 2
BANDS = 64
NX = 32
N_BAND = 8


def draw_visit_blocks(key, part):
    first_key = jax.random.fold_in(key, 11)
    second_key = jax.random.fold_in(key, 23)
    others = jax.random.permutation(first_key, 2 * N_BAND - 1)[:VISITS - 1]
    top_code = jnp.full((1,), 2 * N_BAND - 1, jnp.int32)
    together = jnp.concatenate([others.astype(jnp.int32), top_code], axis=0)
    return jax.random.permutation(second_key, together).astype(jnp.int32)


def spread_offsets(key, first_salt):
    spread_key = jax.random.fold_in(key, first_salt)
    offset = jax.random.uniform(spread_key, (GAUSS,), jnp.float32, -1.0, 1.0)
    return offset


def draw_kernel_rates(key, part):
    offset = spread_offsets(key, 31)
    centres = jnp.array([0.014, 0.4, 2.4], jnp.float32)
    return (centres * jnp.exp(0.35 * offset)).astype(jnp.float32)


def draw_kernel_weights(key, part):
    offset = spread_offsets(key, 41)
    centres = jnp.array([0.1, 0.35, 1.0], jnp.float32)
    return (centres * jnp.exp(0.35 * offset)).astype(jnp.float32)


def block_scale(key, shape, shards, low, largest):
    loudness, own = 1.0, jax.random.fold_in(key, 6)
    for axis_at, shards_of in shards:
        draws = jnp.exp(jax.random.uniform(jax.random.fold_in(own, axis_at), (shards_of,), jnp.float32, low / len(shards), largest / len(shards)))
        loudness = loudness * jnp.repeat(draws, shape[axis_at] // shards_of).reshape([-1 if axis == axis_at else 1 for axis in range(len(shape))])
    return loudness


def scatter_about(key, shape, deviation, reach, shards=(), held_as=jnp.bfloat16):
    entries = jax.random.normal(key, shape, jnp.float32) * deviation
    if len(shards) > 0:
        entries = block_scale(key, shape, shards, -0.22, 0.18) * entries
    return jnp.clip(entries, min=-reach, max=reach).astype(held_as)


def setup_inputs(seed: int = 0) -> dict:
    streams_of = jax.random.split(jax.random.key(seed), 5)
    orbitals = scatter_about(streams_of[0], (BANDS, NX, CY, CZ), 1.0, 6.0, ((0, 8), (1, 16)))
    visit_blocks = draw_visit_blocks(jax.random.fold_in(streams_of[4], 71), 0)
    kernel_rates = draw_kernel_rates(jax.random.fold_in(streams_of[4], 71), 0)
    kernel_weights = draw_kernel_weights(jax.random.fold_in(streams_of[4], 71), 0)
    return {"orbitals": orbitals, "visit_blocks": visit_blocks, "kernel_rates": kernel_rates, "kernel_weights": kernel_weights}


def make_taps(kernel_rates):
    offsets = jnp.arange(-REACH, REACH + 1).astype(jnp.float32)
    return jnp.exp(-kernel_rates[:, None] * (offsets * offsets)[None, :])


def pad_axis(values_in, axis_index):
    widths = [(0, 0)] * values_in.ndim
    widths[axis_index] = (REACH, REACH)
    return jnp.pad(values_in, widths)


def line_pass(values_in, tap_table, axis_index):
    length = values_in.shape[axis_index] - 2 * REACH
    result = None
    for offset in range(2 * REACH + 1):
        shifted = lax.slice_in_dim(values_in, offset, offset + length, axis=axis_index).astype(jnp.float32)
        term = tap_table[:, offset].reshape((-1, 1, 1, 1, 1)) * shifted
        result = term if result is None else result + term
    return result


def accumulate(exchange_sum, padded, visitors, tap_table, kernel_weights, planes):
    for member in range(visitors.shape[0]):
        partner = visitors[member]
        density = (padded.astype(jnp.float32) * partner.astype(jnp.float32)[None]).astype(jnp.bfloat16)
        along_x = line_pass(density[None], tap_table, 2).astype(jnp.bfloat16)
        along_y = line_pass(pad_axis(along_x, 3), tap_table, 3).astype(jnp.bfloat16)
        along_z = line_pass(pad_axis(along_y, 4), tap_table, 4)
        potential = jnp.sum(kernel_weights[:, None, None, None, None] * along_z, axis=0)
        exchange_sum = exchange_sum + potential * partner[REACH:REACH + planes].astype(jnp.float32)[None]
    return exchange_sum


def reference(orbitals, visit_blocks, kernel_rates, kernel_weights):
    tap_table = make_taps(kernel_rates)
    padded = pad_axis(orbitals, 1)
    picked = []
    for visit_index in range(VISITS):
        block_code = visit_blocks[visit_index]
        first_row = ((block_code // 2) * RESIDENT + (block_code % 2) * BLOCK).astype(jnp.int32)
        picked.append(lax.dynamic_slice_in_dim(padded, first_row, BLOCK, 0))
    visitors = jnp.concatenate(picked, axis=0)
    groups = padded.reshape(N_BAND, RESIDENT, NX + 2 * REACH, CY, CZ)

    def one_group(resident):
        start_sum = jnp.zeros((RESIDENT, NX, CY, CZ), jnp.float32)
        return accumulate(start_sum, resident, visitors, tap_table, kernel_weights, NX)

    result = lax.map(one_group, groups)
    return result.reshape(BANDS, NX, CY, CZ)
```

```python
import jax
import jax.numpy as jnp
from jax import lax
from jax.experimental import pallas as pl
from jax.experimental.pallas import tpu as pltpu
from jax.sharding import PartitionSpec as P

BLOCK = 4
VISITS = 2
REACH = 2
GAUSS = 3
CHUNK = 16


def tap_values(rate):
    lane = lax.broadcasted_iota(jnp.int32, (8, 128), 1).astype(jnp.float32)
    scale = 1.0 + lane * (1.0 / 128.0)
    near = jnp.exp(jnp.full((8, 128), -rate))
    far = jnp.exp(jnp.full((8, 128), -4.0 * rate))
    near_error = scale * near - (scale * near).astype(jnp.bfloat16).astype(jnp.float32)
    far_error = scale * far - (scale * far).astype(jnp.bfloat16).astype(jnp.float32)
    cost = (near_error * near_error + far_error * far_error) / (scale * scale)
    best = jnp.min(jnp.where(cost == jnp.min(cost), scale, 4.0))
    return jnp.max(near), jnp.max(far), best


def banded(size, block, scale, near, far):
    row = lax.broadcasted_iota(jnp.int32, (size, size), 0)
    column = lax.broadcasted_iota(jnp.int32, (size, size), 1)
    gap = jnp.abs(row - column)
    taps = jnp.where(gap == 0, scale, jnp.where(gap == 1, scale * near, scale * far))
    keep = gap <= REACH
    if block < size:
        keep = keep & ((row // block) == (column // block))
    return jnp.where(keep, taps, 0.0).astype(jnp.bfloat16)


def pair_kernel(rates, weights, own, low, high, v_own, v_low, v_high, out, lines, y_band, z_band):
    residents, planes, cy, cz = own.shape
    taps = []
    for g in range(GAUSS):
        near, far, scale = tap_values(rates[g])
        taps.append((near, far, weights[g] / (scale * scale)))
        y_band[g] = banded(planes * cy, cy, scale, near, far)
        z_band[g * cz : (g + 1) * cz, :] = banded(cz, cz, scale, near, far)
    out[...] = jnp.zeros_like(out)
    sides = ((low, v_low, 0), (low, v_low, 1), (own, v_own, 0), (own, v_own, 1), (high, v_high, 0), (high, v_high, 1))

    def x_pass(i, j):
        for y in range(0, cy, CHUNK):
            rows = slice(y, y + CHUNK)
            density = [(r[i, p, rows, :] * v[j, p, rows, :]).astype(jnp.float32) for r, v, p in sides]
            for p in range(planes):
                ones = density[p + 1] + density[p + 3]
                twos = density[p] + density[p + 4]
                for g in range(GAUSS):
                    near, far, _ = taps[g]
                    line = density[p + 2] + near * ones + far * twos
                    lines[i, g, p * cy + y : p * cy + y + CHUNK, :] = line.astype(jnp.bfloat16)

    def yz_pass(i, j):
        along = []
        for g in range(GAUSS):
            line = jnp.dot(y_band[g], lines[i, g], preferred_element_type=jnp.float32)
            along.append((line * taps[g][2]).astype(jnp.bfloat16))
        potential = jnp.dot(jnp.concatenate(along, axis=1), z_band[...], preferred_element_type=jnp.float32)
        for p in range(planes):
            out[i, p] += potential[p * cy : (p + 1) * cy] * v_own[j, p].astype(jnp.float32)

    def visitor(j, carry):
        for i in range(residents):
            x_pass(i, j)
            yz_pass(i, j)
        return carry

    lax.fori_loop(0, v_own.shape[0], visitor, 0)


def pairs(rates, weights, *blocks):
    residents, planes, cy, cz = blocks[0].shape
    vmem = pl.BlockSpec(memory_space=pltpu.VMEM)
    smem = pl.BlockSpec(memory_space=pltpu.SMEM)
    return pl.pallas_call(
        pair_kernel,
        out_shape=jax.ShapeDtypeStruct(blocks[0].shape, jnp.float32),
        in_specs=[smem, smem] + [vmem] * 6,
        out_specs=vmem,
        scratch_shapes=[
            pltpu.VMEM((residents, GAUSS, planes * cy, cz), jnp.bfloat16),
            pltpu.VMEM((GAUSS, planes * cy, planes * cy), jnp.bfloat16),
            pltpu.VMEM((GAUSS * cz, cz), jnp.bfloat16),
        ],
        compiler_params=pltpu.CompilerParams(vmem_limit_bytes=48 << 20),
    )(rates, weights, *blocks)


def neighbours(block):
    count = lax.axis_size("dom")
    forward = [(i, i + 1) for i in range(count - 1)]
    backward = [(target, source) for source, target in forward]
    return lax.ppermute(block, "dom", forward), lax.ppermute(block, "dom", backward)


def local(orbitals, visit_blocks, kernel_rates, kernel_weights):
    low, high = neighbours(orbitals)
    picked = []
    for visit_index in range(VISITS):
        code = visit_blocks[visit_index]
        own_block = lax.dynamic_slice_in_dim(orbitals, code % 2 * BLOCK, BLOCK, 0)
        picked.append(jnp.where(lax.axis_index("band") == code // 2, own_block, 0).astype(orbitals.dtype))
    visitors = lax.psum(jnp.concatenate(picked, 0), "band")
    v_low, v_high = neighbours(visitors)
    return pairs(kernel_rates, kernel_weights, orbitals, low, high, visitors, v_low, v_high)


def solution(mesh):
    return jax.shard_map(
        local,
        mesh=mesh,
        in_specs=(P("band", "dom", None, None), P(), P(), P()),
        out_specs=P("band", "dom", None, None),
        check_vma=False,
    )
```

```python
import functools

import jax
import jax.numpy as jnp
from jax import lax
from jax.experimental import pallas as pl
from jax.experimental.pallas import tpu as pltpu
from jax.sharding import PartitionSpec as P

BLOCK = 4
VISITS = 2
REACH = 2
GAUSS = 3
RING = 4
LAST_OWNER = 7
CROSS = (0, 1, 3, 2)
EARLY = 2
MESH = pl.DeviceIdType.MESH
CHUNK = 16


def tap_values(rate):
    lane = lax.broadcasted_iota(jnp.int32, (8, 128), 1).astype(jnp.float32)
    scale = 1.0 + lane * (1.0 / 128.0)
    near = jnp.exp(jnp.full((8, 128), -rate))
    far = jnp.exp(jnp.full((8, 128), -4.0 * rate))
    near_error = scale * near - (scale * near).astype(jnp.bfloat16).astype(jnp.float32)
    far_error = scale * far - (scale * far).astype(jnp.bfloat16).astype(jnp.float32)
    cost = (near_error * near_error + far_error * far_error) / (scale * scale)
    best = jnp.min(jnp.where(cost == jnp.min(cost), scale, 4.0))
    return jnp.max(near), jnp.max(far), best


def banded(size, block, scale, near, far):
    row = lax.broadcasted_iota(jnp.int32, (size, size), 0)
    column = lax.broadcasted_iota(jnp.int32, (size, size), 1)
    gap = jnp.abs(row - column)
    taps = jnp.where(gap == 0, scale, jnp.where(gap == 1, scale * near, scale * far))
    keep = gap <= REACH
    if block < size:
        keep = keep & ((row // block) == (column // block))
    return jnp.where(keep, taps, 0.0).astype(jnp.bfloat16)


def pair_kernel(rates, weights, own, off, par, v_own, v_off, v_par, out, lines, y_band, z_band):
    residents, planes, cy, cz = own.shape
    taps = []
    for g in range(GAUSS):
        near, far, scale = tap_values(rates[g])
        taps.append((near, far, weights[g] / (scale * scale)))
        y_band[g] = banded(planes * cy, cy, scale, near, far)
        z_band[g * cz : (g + 1) * cz, :] = banded(cz, cz, scale, near, far)
    out[...] = jnp.zeros_like(out)
    flip = lax.axis_index("dom") % 2
    plane = (flip, 1 - flip)
    sides = [(r, v, plane[p]) for r, v in ((off, v_off), (own, v_own), (par, v_par)) for p in range(planes)]

    def x_pass(i, j):
        for y in range(0, cy, CHUNK):
            rows = slice(y, y + CHUNK)
            density = [(r[i, p, rows, :] * v[j, p, rows, :]).astype(jnp.float32) for r, v, p in sides]
            for p in range(planes):
                ones = density[p + 1] + density[p + 3]
                twos = density[p] + density[p + 4]
                for g in range(GAUSS):
                    near, far, _ = taps[g]
                    line = density[p + 2] + near * ones + far * twos
                    lines[i, g, p * cy + y : p * cy + y + CHUNK, :] = line.astype(jnp.bfloat16)

    def yz_pass(i, j):
        along = []
        for g in range(GAUSS):
            line = jnp.dot(y_band[g], lines[i, g], preferred_element_type=jnp.float32)
            along.append((line * taps[g][2]).astype(jnp.bfloat16))
        potential = jnp.dot(jnp.concatenate(along, axis=1), z_band[...], preferred_element_type=jnp.float32)
        for p in range(planes):
            out[i, plane[p]] += potential[p * cy : (p + 1) * cy] * v_own[j, plane[p]].astype(jnp.float32)

    def visitor(j, carry):
        for i in range(residents):
            x_pass(i, j)
            yz_pass(i, j)
        return carry

    lax.fori_loop(0, v_own.shape[0], visitor, 0)


def pairs(rates, weights, *blocks):
    residents, planes, cy, cz = blocks[0].shape
    vmem = pl.BlockSpec(memory_space=pltpu.VMEM)
    smem = pl.BlockSpec(memory_space=pltpu.SMEM)
    return pl.pallas_call(
        pair_kernel,
        out_shape=jax.ShapeDtypeStruct(blocks[0].shape, jnp.float32),
        in_specs=[smem, smem] + [vmem] * 6,
        out_specs=vmem,
        scratch_shapes=[
            pltpu.VMEM((residents, GAUSS, planes * cy, cz), jnp.bfloat16),
            pltpu.VMEM((GAUSS, planes * cy, planes * cy), jnp.bfloat16),
            pltpu.VMEM((GAUSS * cz, cz), jnp.bfloat16),
        ],
        compiler_params=pltpu.CompilerParams(vmem_limit_bytes=48 << 20),
    )(rates, weights, *blocks)


def exchange_kernel(owner, orbitals, other, off, par, v_own, v_off, v_par, unit_send, own_recv, off_recv, par_recv,
                    r_send, r_off_recv, r_par_recv, local_sem):
    band, dom = lax.axis_index("band"), lax.axis_index("dom")
    side, place, core = band // RING, band % RING, dom % 2
    up = side * RING + (place + 1) % RING
    down = side * RING + (place + RING - 1) % RING
    twin = (1 - side) * RING + place
    mate = dom + 1 - 2 * core
    away = dom - 1 + 2 * core
    inside = (dom > 0) & (dom < lax.axis_size("dom") - 1)
    yes = dom >= 0

    barrier = pltpu.get_barrier_semaphore()
    for target in (up, down, twin):
        pl.semaphore_signal(barrier, inc=1, device_id={"band": target}, device_id_type=MESH)
    pl.semaphore_signal(barrier, inc=1, device_id={"dom": mate}, device_id_type=MESH)

    @pl.when(inside)
    def _():
        pl.semaphore_signal(barrier, inc=1, device_id={"dom": away}, device_id_type=MESH)
        pl.semaphore_wait(barrier, 5)

    @pl.when(jnp.logical_not(inside))
    def _():
        pl.semaphore_wait(barrier, 4)
        off[...] = jnp.zeros_like(off)
        v_off[...] = jnp.zeros_like(v_off)

    def send(source, target, send_sem, recv_sem, **device):
        return pltpu.make_async_remote_copy(
            src_ref=source, dst_ref=target, send_sem=send_sem, recv_sem=recv_sem, device_id=device, device_id_type=MESH
        )

    def routes(block, m, halo):
        root = (LAST_OWNER, owner)[block]
        row = block * BLOCK + m
        gap = (place + RING - root % RING) % RING
        home = side == root // RING
        step = (gap - CROSS[m] + RING) % RING
        climbs = m < BLOCK // 2
        if climbs:
            go_up, go_down = home & (gap < 3), None
        else:
            go_up, go_down = None, home & (gap != 1)
        far_up = jnp.logical_not(home) & ((step == 0) | (step == 1) if not halo else step == 0)
        far_down = jnp.logical_not(home) & (step == 0 if not halo else (step == 0) | (step == 3))
        go_up = far_up if go_up is None else go_up | far_up
        go_down = far_down if go_down is None else go_down | far_down
        buffer, recv = (v_off, off_recv) if halo else (v_own, own_recv)
        slots = unit_send.at[halo, row]
        first = band == root
        source = orbitals.at[BLOCK + m] if block == 0 else other.at[m]
        plan = []
        for k, (condition, device) in enumerate(
            ((go_up, {"band": up}), (go_down, {"band": down}), (home & (gap == CROSS[m]), {"band": twin}))
        ):
            if halo:
                condition = condition & inside
                plan.append((condition, send(v_off.at[row], v_off.at[row], slots.at[k], recv.at[row], **device)))
            else:
                plan.append((condition & first, send(source, v_own.at[row], slots.at[k], recv.at[row], **device)))
                plan.append(
                    (condition & jnp.logical_not(first), send(v_own.at[row], v_own.at[row], slots.at[k], recv.at[row], **device))
                )
        if not halo:
            plan.append((first, send(source, v_par.at[row], slots.at[3], par_recv.at[row], dom=mate)))
            plan.append((jnp.logical_not(first), send(v_own.at[row], v_par.at[row], slots.at[3], par_recv.at[row], dom=mate)))
            plan.append((first & inside, send(source, v_off.at[row], slots.at[4], off_recv.at[row], dom=away)))
        return first, source, row, plan

    def start(condition, copy):
        @pl.when(condition)
        def _():
            copy.start()

    def finish(condition, copy):
        @pl.when(condition)
        def _():
            copy.wait_send()

    r_away = [send(orbitals.at[i], off.at[i], r_send.at[0, i], r_off_recv.at[i], dom=away) for i in range(2 * BLOCK)]
    r_mate = [send(orbitals.at[i], par.at[i], r_send.at[1, i], r_par_recv.at[i], dom=mate) for i in range(2 * BLOCK)]
    units = [(block, m, halo) for halo in range(2) for m in (0, 2, 1, 3) for block in range(2)]
    plans = [routes(*unit) for unit in units]

    for (block, m, halo), (first, source, row, plan) in zip(units, plans):
        if not halo:
            for condition, copy in plan:
                pass

            @pl.when(first)
            def _(source=source, row=row):
                pltpu.make_async_copy(source, v_own.at[row], local_sem.at[row]).start()

    for (block, m, halo), (first, source, row, plan) in zip(units, plans):
        if not halo:

            @pl.when(first)
            def _(plan=plan):
                for condition, copy in plan:
                    start(condition, copy)

    for i in range(EARLY):
        start(inside, r_away[i])
    for copy in r_mate:
        copy.start()
    waiting = list(r_away[EARLY:])
    for (block, m, halo), (first, source, row, plan) in zip(units, plans):
        if halo:

            @pl.when(inside)
            def _(row=row):
                send(v_off.at[row], v_off.at[row], unit_send.at[1, row, 4], off_recv.at[row], dom=away).wait_recv()

            for condition, copy in plan:
                start(condition, copy)
        else:

            @pl.when(jnp.logical_not(first))
            def _(row=row, plan=plan):
                send(v_own.at[row], v_own.at[row], unit_send.at[0, row, 0], own_recv.at[row], dom=mate).wait_recv()
                for condition, copy in plan:
                    start(condition, copy)

        if waiting:
            start(inside, waiting.pop(0))
    for (block, m, halo), (first, source, row, plan) in zip(units, plans):
        for condition, copy in plan:
            finish(condition, copy)
        if not halo:
            send(v_own.at[row], v_par.at[row], unit_send.at[0, row, 3], par_recv.at[row], dom=mate).wait_recv()

            @pl.when(first)
            def _(source=source, row=row):
                pltpu.make_async_copy(source, v_own.at[row], local_sem.at[row]).wait()

    for i in range(2 * BLOCK):

        @pl.when(inside)
        def _(i=i):
            r_away[i].wait()

        r_mate[i].wait()


def exchange(owner, orbitals, other):
    vmem = pl.BlockSpec(memory_space=pltpu.VMEM)
    anywhere = pl.BlockSpec(memory_space=pl.ANY)
    count = 2 * BLOCK
    dma = pltpu.SemaphoreType.DMA
    return pl.pallas_call(
        functools.partial(exchange_kernel, owner),
        out_shape=[jax.ShapeDtypeStruct(orbitals.shape, orbitals.dtype)] * 5,
        in_specs=[anywhere, anywhere],
        out_specs=[vmem] * 5,
        scratch_shapes=[dma((2, count, 5)), dma((count,)), dma((count,)), dma((count,)), dma((2, count)), dma((count,)),
                        dma((count,)), dma((count,))],
        compiler_params=pltpu.CompilerParams(collective_id=owner, has_side_effects=True, vmem_limit_bytes=16 << 20),
        name="exchange" + str(owner),
    )(orbitals, other)


def local(orbitals, visit_blocks, kernel_rates, kernel_weights):
    last = 2 * LAST_OWNER + 1
    code = jnp.where(visit_blocks[0] == last, visit_blocks[1], visit_blocks[0])
    other = lax.dynamic_slice_in_dim(orbitals, code % 2 * BLOCK, BLOCK, 0)
    branches = [functools.partial(exchange, owner) for owner in range(LAST_OWNER + 1)]
    off, par, v_own, v_off, v_par = lax.switch(code // 2, branches, orbitals, other)
    return pairs(kernel_rates, kernel_weights, orbitals, off, par, v_own, v_off, v_par)


def solution(mesh):
    return jax.shard_map(
        local,
        mesh=mesh,
        in_specs=(P("band", "dom", None, None), P(), P(), P()),
        out_specs=P("band", "dom", None, None),
        check_vma=False,
    )
```

```python
import functools

import jax
import jax.numpy as jnp
from jax import lax
from jax.experimental import pallas as pl
from jax.experimental.pallas import tpu as pltpu
from jax.sharding import PartitionSpec as P

BLOCK = 4
VISITS = 2
REACH = 2
GAUSS = 3
RING = 4
LAST_OWNER = 7
CROSS = (0, 1, 3, 2)
EARLY = 2
TURNS = 10
MESH = pl.DeviceIdType.MESH
CHUNK = 16


def tap_values(rate):
    lane = lax.broadcasted_iota(jnp.int32, (8, 128), 1).astype(jnp.float32)
    scale = 1.0 + lane * (1.0 / 128.0)
    near = jnp.exp(jnp.full((8, 128), -rate))
    far = jnp.exp(jnp.full((8, 128), -4.0 * rate))
    near_error = scale * near - (scale * near).astype(jnp.bfloat16).astype(jnp.float32)
    far_error = scale * far - (scale * far).astype(jnp.bfloat16).astype(jnp.float32)
    cost = (near_error * near_error + far_error * far_error) / (scale * scale)
    best = jnp.min(jnp.where(cost == jnp.min(cost), scale, 4.0))
    return jnp.max(near), jnp.max(far), best


def banded(size, block, scale, near, far):
    row = lax.broadcasted_iota(jnp.int32, (size, size), 0)
    column = lax.broadcasted_iota(jnp.int32, (size, size), 1)
    gap = jnp.abs(row - column)
    taps = jnp.where(gap == 0, scale, jnp.where(gap == 1, scale * near, scale * far))
    keep = gap <= REACH
    if block < size:
        keep = keep & ((row // block) == (column // block))
    return jnp.where(keep, taps, 0.0).astype(jnp.bfloat16)


def pair_kernel(rates, weights, own, off, par, v_own, v_off, v_par, out, lines, y_band, z_band):
    residents, planes, cy, cz = own.shape
    taps = []
    for g in range(GAUSS):
        near, far, scale = tap_values(rates[g])
        taps.append((near, far, weights[g] / (scale * scale)))
        y_band[g] = banded(planes * cy, cy, scale, near, far)
        z_band[g * cz : (g + 1) * cz, :] = banded(cz, cz, scale, near, far)
    out[...] = jnp.zeros_like(out)
    flip = lax.axis_index("dom") % 2
    plane = (flip, 1 - flip)
    sides = [(r, v, plane[p]) for r, v in ((off, v_off), (own, v_own), (par, v_par)) for p in range(planes)]

    def x_pass(i, j):
        for y in range(0, cy, CHUNK):
            rows = slice(y, y + CHUNK)
            density = [(r[i, p, rows, :] * v[j, p, rows, :]).astype(jnp.float32) for r, v, p in sides]
            for p in range(planes):
                ones = density[p + 1] + density[p + 3]
                twos = density[p] + density[p + 4]
                for g in range(GAUSS):
                    near, far, _ = taps[g]
                    line = density[p + 2] + near * ones + far * twos
                    lines[i, g, p * cy + y : p * cy + y + CHUNK, :] = line.astype(jnp.bfloat16)

    def yz_pass(i, j):
        along = []
        for g in range(GAUSS):
            line = jnp.dot(y_band[g], lines[i, g], preferred_element_type=jnp.float32)
            along.append((line * taps[g][2]).astype(jnp.bfloat16))
        potential = jnp.dot(jnp.concatenate(along, axis=1), z_band[...], preferred_element_type=jnp.float32)
        for p in range(planes):
            out[i, plane[p]] += potential[p * cy : (p + 1) * cy] * v_own[j, plane[p]].astype(jnp.float32)

    def visitor(j, carry):
        for i in range(residents):
            x_pass(i, j)
            yz_pass(i, j)
        return carry

    lax.fori_loop(0, v_own.shape[0], visitor, 0)


def pairs(rates, weights, *blocks):
    residents, planes, cy, cz = blocks[0].shape
    vmem = pl.BlockSpec(memory_space=pltpu.VMEM)
    smem = pl.BlockSpec(memory_space=pltpu.SMEM)
    return pl.pallas_call(
        pair_kernel,
        out_shape=jax.ShapeDtypeStruct(blocks[0].shape, jnp.float32),
        in_specs=[smem, smem] + [vmem] * 6,
        out_specs=vmem,
        scratch_shapes=[
            pltpu.VMEM((residents, GAUSS, planes * cy, cz), jnp.bfloat16),
            pltpu.VMEM((GAUSS, planes * cy, planes * cy), jnp.bfloat16),
            pltpu.VMEM((GAUSS * cz, cz), jnp.bfloat16),
        ],
        compiler_params=pltpu.CompilerParams(vmem_limit_bytes=48 << 20),
    )(rates, weights, *blocks)


def exchange_kernel(owner, orbitals, other, off, par, v_own, v_off, v_par, unit_send, own_recv, off_recv, par_recv,
                    r_send, r_off_recv, r_par_recv, local_sem):
    band, dom = lax.axis_index("band"), lax.axis_index("dom")
    side, place, core = band // RING, band % RING, dom % 2
    up = side * RING + (place + 1) % RING
    down = side * RING + (place + RING - 1) % RING
    twin = (1 - side) * RING + place
    mate = dom + 1 - 2 * core
    away = dom - 1 + 2 * core
    inside = (dom > 0) & (dom < lax.axis_size("dom") - 1)
    yes = dom >= 0

    barrier = pltpu.get_barrier_semaphore()
    for target in (up, down, twin):
        pl.semaphore_signal(barrier, inc=1, device_id={"band": target}, device_id_type=MESH)
    pl.semaphore_signal(barrier, inc=1, device_id={"dom": mate}, device_id_type=MESH)

    @pl.when(inside)
    def _():
        pl.semaphore_signal(barrier, inc=1, device_id={"dom": away}, device_id_type=MESH)
        pl.semaphore_wait(barrier, 5)

    @pl.when(jnp.logical_not(inside))
    def _():
        pl.semaphore_wait(barrier, 4)
        off[...] = jnp.zeros_like(off)
        v_off[...] = jnp.zeros_like(v_off)

    def send(source, target, send_sem, recv_sem, **device):
        return pltpu.make_async_remote_copy(
            src_ref=source, dst_ref=target, send_sem=send_sem, recv_sem=recv_sem, device_id=device, device_id_type=MESH
        )

    def routes(block, m, halo):
        root = (LAST_OWNER, owner)[block]
        row = block * BLOCK + m
        gap = (place + RING - root % RING) % RING
        home = side == root // RING
        step = (gap - CROSS[m] + RING) % RING
        climbs = m < BLOCK // 2
        if climbs:
            go_up, go_down = home & (gap < 3), None
        else:
            go_up, go_down = None, home & (gap != 1)
        far_up = jnp.logical_not(home) & ((step == 0) | (step == 1) if not halo else step == 0)
        far_down = jnp.logical_not(home) & (step == 0 if not halo else (step == 0) | (step == 3))
        go_up = far_up if go_up is None else go_up | far_up
        go_down = far_down if go_down is None else go_down | far_down
        if climbs:
            depth = gap
        else:
            depth = (RING - gap) % RING
        spread = jnp.where(step == 0, 0, jnp.where(step == 2, 2, 1))
        depth = jnp.where(home, depth, (0, 1, 1, 2)[m] + 1 + spread)
        turn = depth + m % 2 + 3 * halo
        buffer, recv = (v_off, off_recv) if halo else (v_own, own_recv)
        slots = unit_send.at[halo, row]
        first = band == root
        source = orbitals.at[BLOCK + m] if block == 0 else other.at[m]
        plan = []
        for k, (condition, device) in enumerate(
            ((go_up, {"band": up}), (go_down, {"band": down}), (home & (gap == CROSS[m]), {"band": twin}))
        ):
            if halo:
                condition = condition & inside
                plan.append((condition, send(v_off.at[row], v_off.at[row], slots.at[k], recv.at[row], **device)))
            else:
                plan.append((condition & first, send(source, v_own.at[row], slots.at[k], recv.at[row], **device)))
                plan.append(
                    (condition & jnp.logical_not(first), send(v_own.at[row], v_own.at[row], slots.at[k], recv.at[row], **device))
                )
        if not halo:
            plan.append((first, send(source, v_par.at[row], slots.at[3], par_recv.at[row], dom=mate)))
            plan.append((jnp.logical_not(first), send(v_own.at[row], v_par.at[row], slots.at[3], par_recv.at[row], dom=mate)))
            plan.append((first & inside, send(source, v_off.at[row], slots.at[4], off_recv.at[row], dom=away)))
        return first, source, row, plan, turn

    def start(condition, copy):
        @pl.when(condition)
        def _():
            copy.start()

    def finish(condition, copy):
        @pl.when(condition)
        def _():
            copy.wait_send()

    r_away = [send(orbitals.at[i], off.at[i], r_send.at[0, i], r_off_recv.at[i], dom=away) for i in range(2 * BLOCK)]
    r_mate = [send(orbitals.at[i], par.at[i], r_send.at[1, i], r_par_recv.at[i], dom=mate) for i in range(2 * BLOCK)]
    units = [(block, m, halo) for halo in range(2) for m in (0, 2, 1, 3) for block in range(2)]
    plans = [routes(*unit) for unit in units]

    for (block, m, halo), (first, source, row, plan, turn) in zip(units, plans):
        if not halo:

            @pl.when(first)
            def _(source=source, row=row):
                pltpu.make_async_copy(source, v_own.at[row], local_sem.at[row]).start()

    for (block, m, halo), (first, source, row, plan, turn) in zip(units, plans):
        if not halo:

            @pl.when(first)
            def _(plan=plan):
                for condition, copy in plan:
                    start(condition, copy)

    for i in range(EARLY):
        start(inside, r_away[i])
    for copy in r_mate:
        copy.start()
    def advance(now, carry):
        for (block, m, halo), (first, source, row, plan, turn) in zip(units, plans):
            arrives = inside if halo else jnp.logical_not(first)

            @pl.when(arrives & (turn == now))
            def _(halo=halo, row=row, plan=plan):
                buffer, recv = (v_off, off_recv) if halo else (v_own, own_recv)
                send(buffer.at[row], buffer.at[row], unit_send.at[halo, row, 0], recv.at[row], dom=mate).wait_recv()
                for condition, copy in plan:
                    start(condition, copy)

        @pl.when(inside & (now < 2 * BLOCK - EARLY))
        def _():
            i = EARLY + now
            send(orbitals.at[i], off.at[i], r_send.at[0, i], r_off_recv.at[i], dom=away).start()

        return carry

    lax.fori_loop(0, TURNS, advance, 0)
    for (block, m, halo), (first, source, row, plan, turn) in zip(units, plans):
        for condition, copy in plan:
            finish(condition, copy)
        if not halo:
            send(v_own.at[row], v_par.at[row], unit_send.at[0, row, 3], par_recv.at[row], dom=mate).wait_recv()

            @pl.when(first)
            def _(source=source, row=row):
                pltpu.make_async_copy(source, v_own.at[row], local_sem.at[row]).wait()

    for i in range(2 * BLOCK):

        @pl.when(inside)
        def _(i=i):
            r_away[i].wait()

        r_mate[i].wait()


def exchange(owner, orbitals, other):
    vmem = pl.BlockSpec(memory_space=pltpu.VMEM)
    anywhere = pl.BlockSpec(memory_space=pl.ANY)
    count = 2 * BLOCK
    dma = pltpu.SemaphoreType.DMA
    return pl.pallas_call(
        functools.partial(exchange_kernel, owner),
        out_shape=[jax.ShapeDtypeStruct(orbitals.shape, orbitals.dtype)] * 5,
        in_specs=[anywhere, anywhere],
        out_specs=[vmem] * 5,
        scratch_shapes=[dma((2, count, 5)), dma((count,)), dma((count,)), dma((count,)), dma((2, count)), dma((count,)),
                        dma((count,)), dma((count,))],
        compiler_params=pltpu.CompilerParams(collective_id=owner, has_side_effects=True, vmem_limit_bytes=16 << 20),
        name="exchange" + str(owner),
    )(orbitals, other)


def local(orbitals, visit_blocks, kernel_rates, kernel_weights):
    last = 2 * LAST_OWNER + 1
    code = jnp.where(visit_blocks[0] == last, visit_blocks[1], visit_blocks[0])
    other = lax.dynamic_slice_in_dim(orbitals, code % 2 * BLOCK, BLOCK, 0)
    branches = [functools.partial(exchange, owner) for owner in range(LAST_OWNER + 1)]
    off, par, v_own, v_off, v_par = lax.switch(code // 2, branches, orbitals, other)
    return pairs(kernel_rates, kernel_weights, orbitals, off, par, v_own, v_off, v_par)


def solution(mesh):
    return jax.shard_map(
        local,
        mesh=mesh,
        in_specs=(P("band", "dom", None, None), P(), P(), P()),
        out_specs=P("band", "dom", None, None),
        check_vma=False,
    )
```

```python
import functools

import jax
import jax.numpy as jnp
from jax import lax
from jax.experimental import pallas as pl
from jax.experimental.pallas import tpu as pltpu
from jax.sharding import PartitionSpec as P

BLOCK = 4
VISITS = 2
REACH = 2
GAUSS = 3
RING = 4
LAST_OWNER = 7
EARLY = 0
TURNS = 16
SCHEDULES = (
    (
        (10524161, 106601, 7864528, 45133, 4915226, 2364802, 14685824, 6818946, 5833408, 45071, 6833155, 106601, 15205889, 6817803, 10524288, 4206607),
        (67114086, 3072741376, 269644379, 3643908881, 558431101, 2783772978, 844314537, 2329683331, 1131137231, 2608154148, 1451548634, 4238272837, 1756859132, 3456068759, 2143993326, 4004093624),
    ),
    (
        (5832912, 4207638, 2150411, 361522, 15206016, 852808, 13174273, 106616, 10524161, 2392680, 2151427, 852808, 7344336, 4206622, 15206016, 106554),
        (1401482, 2321683712, 354450835, 2734901521, 557908900, 2492211237, 844707831, 3073855794, 1284803769, 3380515916, 1589047259, 3958359646, 1725496271, 3757811814, 2026553069, 4256029304),
    ),
    (
        (2151427, 852801, 6426712, 2884417, 13174400, 45206, 14685328, 106736, 10523145, 106674, 2151427, 6818369, 5833408, 2884048, 14685824, 2884048),
        (83921490, 1628700720, 270662763, 2489983365, 574035827, 2930070017, 861030846, 3645453076, 1265860297, 4253795366, 1606873066, 3170657703, 1990056927, 3351156296, 2296954364, 3940526237),
    ),
    (
        (2150411, 4787344, 2150411, 45581, 7864528, 853392, 5833281, 46597, 2150411, 6818313, 5833408, 2885008, 14685697, 4208260, 14685824, 6819456),
        (50366786, 1112080388, 371309957, 2840794128, 538088282, 3026985255, 825738989, 3734319665, 1551167417, 2614840419, 1703869135, 3938407804, 2007411675, 4293552022, 2294865662, 3455940776),
    ),
    (
        (10524288, 430106, 10524161, 430168, 5832912, 4744195, 7864528, 4743179, 10524288, 4743179, 2150411, 176216, 10524288, 13116929, 7865024, 4744195),
        (104071201, 2986369539, 408228708, 3557926454, 539771225, 1130505488, 826836092, 1434671170, 1822111655, 2848365973, 2126376923, 3396860813, 2413722346, 3957964030, 2544884175, 4261072568),
    ),
    (
        (10524161, 491546, 2150411, 4399130, 7865024, 10782336, 15205889, 1409232, 13174400, 2523224, 2151427, 4284427, 5833408, 4399192, 15206016, 237656),
        (139460640, 1342251265, 445798738, 2568192787, 560218696, 2183817963, 866522228, 3023402380, 1171077014, 3327039029, 1860755418, 3715612343, 2011154639, 4018793321, 2885463293, 4240178606),
    ),
    (
        (10524161, 868363, 2265176, 3412176, 7344832, 983066, 13174273, 615427, 13174400, 3412176, 6311947, 10753664, 5832912, 983066, 14685697, 1900752),
        (186646816, 1073896017, 490850119, 1367678980, 610484792, 2182382611, 894966642, 3812015781, 1790850454, 3068883821, 2091380681, 3355286780, 2665470430, 3631938955, 2949212394, 4187793087),
    ),
    (
        (2265176, 2151427, 10524161, 2150411, 2150411, 5832912, 4915288, 5833408, 2151427, 10524288, 10524161, 4915288, 5832912, 5832912, 15206016, 15205889),
        (50365444, 354497841, 658636816, 962820707, 1267056311, 1343496485, 1630979912, 1918390873, 2376589274, 2663977842, 2951432358, 3027958924, 3332150941, 3636390351, 3940379627, 4244614654),
    ),
)
MESH = pl.DeviceIdType.MESH
CHUNK = 16


def tap_values(rate):
    lane = lax.broadcasted_iota(jnp.int32, (8, 128), 1).astype(jnp.float32)
    scale = 1.0 + lane * (1.0 / 128.0)
    near = jnp.exp(jnp.full((8, 128), -rate))
    far = jnp.exp(jnp.full((8, 128), -4.0 * rate))
    near_error = scale * near - (scale * near).astype(jnp.bfloat16).astype(jnp.float32)
    far_error = scale * far - (scale * far).astype(jnp.bfloat16).astype(jnp.float32)
    cost = (near_error * near_error + far_error * far_error) / (scale * scale)
    best = jnp.min(jnp.where(cost == jnp.min(cost), scale, 4.0))
    return jnp.max(near), jnp.max(far), best


def banded(size, block, scale, near, far):
    row = lax.broadcasted_iota(jnp.int32, (size, size), 0)
    column = lax.broadcasted_iota(jnp.int32, (size, size), 1)
    gap = jnp.abs(row - column)
    taps = jnp.where(gap == 0, scale, jnp.where(gap == 1, scale * near, scale * far))
    keep = gap <= REACH
    if block < size:
        keep = keep & ((row // block) == (column // block))
    return jnp.where(keep, taps, 0.0).astype(jnp.bfloat16)


def pair_kernel(rates, weights, own, off, par, v_own, v_off, v_par, out, lines, y_band, z_band):
    residents, planes, cy, cz = own.shape
    taps = []
    for g in range(GAUSS):
        near, far, scale = tap_values(rates[g])
        taps.append((near, far, weights[g] / (scale * scale)))
        y_band[g] = banded(planes * cy, cy, scale, near, far)
        z_band[g * cz : (g + 1) * cz, :] = banded(cz, cz, scale, near, far)
    out[...] = jnp.zeros_like(out)
    flip = lax.axis_index("dom") % 2
    plane = (flip, 1 - flip)
    sides = [(r, v, plane[p]) for r, v in ((off, v_off), (own, v_own), (par, v_par)) for p in range(planes)]

    def x_pass(i, j):
        for y in range(0, cy, CHUNK):
            rows = slice(y, y + CHUNK)
            density = [(r[i, p, rows, :] * v[j, p, rows, :]).astype(jnp.float32) for r, v, p in sides]
            for p in range(planes):
                ones = density[p + 1] + density[p + 3]
                twos = density[p] + density[p + 4]
                for g in range(GAUSS):
                    near, far, _ = taps[g]
                    line = density[p + 2] + near * ones + far * twos
                    lines[i, g, p * cy + y : p * cy + y + CHUNK, :] = line.astype(jnp.bfloat16)

    def yz_pass(i, j):
        along = []
        for g in range(GAUSS):
            line = jnp.dot(y_band[g], lines[i, g], preferred_element_type=jnp.float32)
            along.append((line * taps[g][2]).astype(jnp.bfloat16))
        potential = jnp.dot(jnp.concatenate(along, axis=1), z_band[...], preferred_element_type=jnp.float32)
        for p in range(planes):
            out[i, plane[p]] += potential[p * cy : (p + 1) * cy] * v_own[j, plane[p]].astype(jnp.float32)

    def visitor(j, carry):
        for i in range(residents):
            x_pass(i, j)
            yz_pass(i, j)
        return carry

    lax.fori_loop(0, v_own.shape[0], visitor, 0)


def pairs(rates, weights, *blocks):
    residents, planes, cy, cz = blocks[0].shape
    vmem = pl.BlockSpec(memory_space=pltpu.VMEM)
    smem = pl.BlockSpec(memory_space=pltpu.SMEM)
    return pl.pallas_call(
        pair_kernel,
        out_shape=jax.ShapeDtypeStruct(blocks[0].shape, jnp.float32),
        in_specs=[smem, smem] + [vmem] * 6,
        out_specs=vmem,
        scratch_shapes=[
            pltpu.VMEM((residents, GAUSS, planes * cy, cz), jnp.bfloat16),
            pltpu.VMEM((GAUSS, planes * cy, planes * cy), jnp.bfloat16),
            pltpu.VMEM((GAUSS * cz, cz), jnp.bfloat16),
        ],
        compiler_params=pltpu.CompilerParams(vmem_limit_bytes=48 << 20),
    )(rates, weights, *blocks)


def exchange_kernel(owner, orbitals, other, off, par, v_own, v_off, v_par, unit_send, own_recv, off_recv, par_recv,
                    r_send, r_off_recv, r_par_recv, local_sem):
    band, dom = lax.axis_index("band"), lax.axis_index("dom")
    side, place, core = band // RING, band % RING, dom % 2
    up = side * RING + (place + 1) % RING
    down = side * RING + (place + RING - 1) % RING
    twin = (1 - side) * RING + place
    mate = dom + 1 - 2 * core
    away = dom - 1 + 2 * core
    inside = (dom > 0) & (dom < lax.axis_size("dom") - 1)
    yes = dom >= 0

    barrier = pltpu.get_barrier_semaphore()
    for target in (up, down, twin):
        pl.semaphore_signal(barrier, inc=1, device_id={"band": target}, device_id_type=MESH)
    pl.semaphore_signal(barrier, inc=1, device_id={"dom": mate}, device_id_type=MESH)

    @pl.when(inside)
    def _():
        pl.semaphore_signal(barrier, inc=1, device_id={"dom": away}, device_id_type=MESH)
        pl.semaphore_wait(barrier, 5)

    @pl.when(jnp.logical_not(inside))
    def _():
        pl.semaphore_wait(barrier, 4)
        off[...] = jnp.zeros_like(off)
        v_off[...] = jnp.zeros_like(v_off)

    def send(source, target, send_sem, recv_sem, **device):
        return pltpu.make_async_remote_copy(
            src_ref=source, dst_ref=target, send_sem=send_sem, recv_sem=recv_sem, device_id=device, device_id_type=MESH
        )

    def by_band(packed, base):
        value = 0
        for k in range(lax.axis_size("band")):
            value = jnp.where(band == k, packed // base**k % base, value)
        return value

    def routes(block, m, halo):
        root = (LAST_OWNER, owner)[block]
        row = block * BLOCK + m
        number = (halo * BLOCK + m) * 2 + block
        flags = by_band(SCHEDULES[owner][0][number], 8)
        turn = by_band(SCHEDULES[owner][1][number], 16)
        buffer, recv = (v_off, off_recv) if halo else (v_own, own_recv)
        slots = unit_send.at[halo, row]
        first = band == root
        source = orbitals.at[BLOCK + m] if block == 0 else other.at[m]
        plan = []
        for k, (condition, device) in enumerate(
            ((flags % 2 == 1, {"band": up}), (flags // 2 % 2 == 1, {"band": down}), (flags // 4 == 1, {"band": twin}))
        ):
            if halo:
                condition = condition & inside
                plan.append((condition, send(v_off.at[row], v_off.at[row], slots.at[k], recv.at[row], **device)))
            else:
                plan.append((condition & first, send(source, v_own.at[row], slots.at[k], recv.at[row], **device)))
                plan.append(
                    (condition & jnp.logical_not(first), send(v_own.at[row], v_own.at[row], slots.at[k], recv.at[row], **device))
                )
        if not halo:
            plan.append((first, send(source, v_par.at[row], slots.at[3], par_recv.at[row], dom=mate)))
            plan.append((jnp.logical_not(first), send(v_own.at[row], v_par.at[row], slots.at[3], par_recv.at[row], dom=mate)))
            plan.append((first & inside, send(source, v_off.at[row], slots.at[4], off_recv.at[row], dom=away)))
        return first, source, row, plan, turn

    def start(condition, copy):
        @pl.when(condition)
        def _():
            copy.start()

    def finish(condition, copy):
        @pl.when(condition)
        def _():
            copy.wait_send()

    r_away = [send(orbitals.at[i], off.at[i], r_send.at[0, i], r_off_recv.at[i], dom=away) for i in range(2 * BLOCK)]
    r_mate = [send(orbitals.at[i], par.at[i], r_send.at[1, i], r_par_recv.at[i], dom=mate) for i in range(2 * BLOCK)]
    units = [(block, m, halo) for halo in range(2) for m in range(BLOCK) for block in range(2)]
    plans = [routes(*unit) for unit in units]

    for (block, m, halo), (first, source, row, plan, turn) in zip(units, plans):
        if not halo:

            @pl.when(first)
            def _(source=source, row=row):
                pltpu.make_async_copy(source, v_own.at[row], local_sem.at[row]).start()

    for (block, m, halo), (first, source, row, plan, turn) in zip(units, plans):
        if not halo:

            @pl.when(first)
            def _(plan=plan):
                for condition, copy in plan[6:]:
                    start(condition, copy)

    for i in range(EARLY):
        start(inside, r_away[i])
    for copy in r_mate:
        copy.start()
    def advance(now, carry):
        for (block, m, halo), (first, source, row, plan, turn) in zip(units, plans):
            arrives = inside if halo else jnp.logical_not(first)

            @pl.when(turn == now)
            def _(halo=halo, row=row, plan=plan, arrives=arrives):
                buffer, recv = (v_off, off_recv) if halo else (v_own, own_recv)

                @pl.when(arrives)
                def _():
                    send(buffer.at[row], buffer.at[row], unit_send.at[halo, row, 0], recv.at[row], dom=mate).wait_recv()

                for condition, copy in plan if halo else plan[:6]:
                    start(condition, copy)
                if not halo:
                    start(*plan[7])

        @pl.when(inside & (now < 2 * BLOCK - EARLY))
        def _():
            i = EARLY + now
            send(orbitals.at[i], off.at[i], r_send.at[0, i], r_off_recv.at[i], dom=away).start()

        return carry

    lax.fori_loop(0, TURNS, advance, 0)
    for (block, m, halo), (first, source, row, plan, turn) in zip(units, plans):
        for condition, copy in plan:
            finish(condition, copy)
        if not halo:
            send(v_own.at[row], v_par.at[row], unit_send.at[0, row, 3], par_recv.at[row], dom=mate).wait_recv()

            @pl.when(first)
            def _(source=source, row=row):
                pltpu.make_async_copy(source, v_own.at[row], local_sem.at[row]).wait()

    for i in range(2 * BLOCK):

        @pl.when(inside)
        def _(i=i):
            r_away[i].wait()

        r_mate[i].wait()


def exchange(owner, orbitals, other):
    vmem = pl.BlockSpec(memory_space=pltpu.VMEM)
    anywhere = pl.BlockSpec(memory_space=pl.ANY)
    count = 2 * BLOCK
    dma = pltpu.SemaphoreType.DMA
    return pl.pallas_call(
        functools.partial(exchange_kernel, owner),
        out_shape=[jax.ShapeDtypeStruct(orbitals.shape, orbitals.dtype)] * 5,
        in_specs=[anywhere, anywhere],
        out_specs=[vmem] * 5,
        scratch_shapes=[dma((2, count, 5)), dma((count,)), dma((count,)), dma((count,)), dma((2, count)), dma((count,)),
                        dma((count,)), dma((count,))],
        compiler_params=pltpu.CompilerParams(collective_id=owner, has_side_effects=True, vmem_limit_bytes=16 << 20),
        name="exchange" + str(owner),
    )(orbitals, other)


def local(orbitals, visit_blocks, kernel_rates, kernel_weights):
    last = 2 * LAST_OWNER + 1
    code = jnp.where(visit_blocks[0] == last, visit_blocks[1], visit_blocks[0])
    other = lax.dynamic_slice_in_dim(orbitals, code % 2 * BLOCK, BLOCK, 0)
    branches = [functools.partial(exchange, owner) for owner in range(LAST_OWNER + 1)]
    off, par, v_own, v_off, v_par = lax.switch(code // 2, branches, orbitals, other)
    return pairs(kernel_rates, kernel_weights, orbitals, off, par, v_own, v_off, v_par)


def solution(mesh):
    return jax.shard_map(
        local,
        mesh=mesh,
        in_specs=(P("band", "dom", None, None), P(), P(), P()),
        out_specs=P("band", "dom", None, None),
        check_vma=False,
    )
```
